256 devices in a mesh: segment: 4 (over z_hi), tp: 16 (over z_lo, x, core), dp: 4 (over y).
Axes of the slice: x: 4, y: 4, z: 8 (z_hi: 4, z_lo: 2; z = z_hi * 2 + z_lo), core: 2. Of those that a mesh axis runs over, the one named last changes fastest.
Arguments:
- inputs: bfloat16 [2, 256, 4096], P(None, 'dp', 'tp'), may hold values from -6 to 6
- cotangent: bfloat16 [2, 256, 4096], P(None, 'dp', 'tp'), may hold values from -6 to 6
- w_in: bfloat16 [4, 4096, 8192], P('segment', None, 'tp'), may hold values from -0.09375 to 0.09375
- w_out: bfloat16 [4, 8192, 4096], P('segment', 'tp'), may hold values from -0.0625 to 0.0625
Outputs:
- segment_grads: bfloat16 [4, 2, 256, 4096], P('segment', None, 'dp', 'tp')
- grad_in: bfloat16 [4, 4096, 8192], P('segment', 'dp', 'tp')
- grad_out: bfloat16 [4, 8192, 4096], P('segment', 'tp', 'dp')
The draws below stay inside these ranges and needn't reach their ends.
All inputs are finite; a program needn't handle non-finite values.
Results may differ from the reference program's by a relative error of at most 0.035.
Values may be sent and summed in bfloat16 or wider, within the bound.
No kernel may reach another device: no remote copies, remote signals or barrier semaphores. Data moves between devices by JAX's collectives and lax.ppermute only.
A program may use at most 64 MiB of HBM per device.

```python
import math
import jax
import jax.numpy as jnp
from jax import lax

D = 4096
FF = 8192
MICRO = 2
SECTIONS = 4
TOTAL_ROWS = 256
N_SEGMENT = 4
N_TP = 16
N_DP = 4


def levels(rng, dims, cuts, low, high):
    def one(dim, parts):
        heights = jax.random.uniform(jax.random.fold_in(jax.random.fold_in(rng, 6), dim), (parts,), jnp.float32, low / len(cuts), high / len(cuts))
        return jnp.repeat(jnp.exp(heights), dims[dim] // parts).reshape((-1,) + (1,) * (len(dims) - dim - 1))

    loudness = one(*cuts[0])
    for cut in cuts[1:]:
        loudness = loudness * one(*cut)
    return loudness


def scatter_about(rng, extent, spread, bound, split=(), held_as=jnp.bfloat16):
    values = jax.random.normal(rng, extent, jnp.float32) * spread
    if len(split) > 0:
        values = levels(rng, extent, split, -0.22, 0.18) * values
    return jnp.clip(values, min=-bound, max=bound).astype(held_as)


def setup_inputs(seed: int = 0) -> dict:
    keys = jax.random.split(jax.random.key(seed), 5)
    inputs = scatter_about(keys[0], (MICRO, TOTAL_ROWS, D), 1.0, 6.0, ((1, 4), (2, 16)))
    cotangent = scatter_about(keys[1], (MICRO, TOTAL_ROWS, D), 1.0, 6.0, ((1, 4), (2, 16)))
    w_in = scatter_about(keys[2], (SECTIONS, D, FF), D ** -0.5, 0.09375, ((0, 4), (2, 16)))
    w_out = scatter_about(keys[3], (SECTIONS, FF, D), FF ** -0.5, 0.0625, ((0, 4), (1, 16)))
    return dict(inputs=inputs, cotangent=cotangent, w_in=w_in, w_out=w_out)


def gelu_pair(pre_act):
    inner_arg = 0.7978845608028654 * (pre_act + 0.044715 * pre_act * pre_act * pre_act)
    tangent = jnp.tanh(inner_arg)
    gelu_value = 0.5 * pre_act * (1.0 + tangent)
    gelu_slope = 0.5 * (1.0 + tangent) + 0.5 * pre_act * (1.0 - tangent * tangent) * 0.7978845608028654 * (1.0 + 3.0 * 0.044715 * pre_act * pre_act)
    return (gelu_value, gelu_slope)

def rounded_sum(part_terms):
    return lax.optimization_barrier(jnp.sum(lax.optimization_barrier(part_terms.astype(jnp.bfloat16)).astype(jnp.float32), axis=0))

def reference(inputs, cotangent, w_in, w_out):
    total_rows = inputs.shape[1]
    unit_block = FF // N_TP
    group_rows = total_rows // N_DP
    factor = 1.0 / math.sqrt(MICRO * total_rows)
    states = [inputs[micro_index] for micro_index in range(MICRO)]
    saved_in = []
    saved_pre = []
    for section in range(N_SEGMENT):
        first_weight = w_in[section]
        stacked_second = w_out[section].reshape(N_TP, unit_block, D).astype(jnp.float32)
        pres = []
        nexts = []
        for micro_index in range(MICRO):
            state_now = states[micro_index]
            pre_act = jnp.dot(state_now, first_weight, preferred_element_type=jnp.float32)
            activation = gelu_pair(pre_act)[0].astype(jnp.bfloat16)
            part_terms = jnp.einsum('rpf,pfd->prd', activation.reshape(total_rows, N_TP, unit_block).astype(jnp.float32), stacked_second)
            nexts.append((state_now.astype(jnp.float32) + rounded_sum(part_terms)).astype(jnp.bfloat16))
            pres.append(pre_act)
        saved_in.append(states)
        saved_pre.append(pres)
        states = nexts
    grads = [cotangent[micro_index] for micro_index in range(MICRO)]
    segment_list = [None] * N_SEGMENT
    first_list = [None] * N_SEGMENT
    second_list = [None] * N_SEGMENT
    for section in reversed(range(N_SEGMENT)):
        first_weight = w_in[section]
        second_weight = w_out[section]
        stacked_first = first_weight.reshape(D, N_TP, unit_block).astype(jnp.float32)
        deltas = []
        activations = []
        news = []
        for micro_index in range(MICRO):
            grad_now = grads[micro_index]
            gelu_value, gelu_slope = gelu_pair(saved_pre[section][micro_index])
            upstream = lax.dot_general(grad_now, second_weight, (((1,), (1,)), ((), ())), preferred_element_type=jnp.float32)
            delta = (upstream * gelu_slope).astype(jnp.bfloat16)
            part_terms = jnp.einsum('rpf,dpf->prd', delta.reshape(total_rows, N_TP, unit_block).astype(jnp.float32), stacked_first)
            news.append((grad_now.astype(jnp.float32) + rounded_sum(part_terms)).astype(jnp.bfloat16))
            deltas.append(delta)
            activations.append(gelu_value.astype(jnp.bfloat16))
        in_all = jnp.stack(saved_in[section]).reshape(MICRO, N_DP, group_rows, D)
        delta_all = jnp.stack(deltas).reshape(MICRO, N_DP, group_rows, FF)
        act_all = jnp.stack(activations).reshape(MICRO, N_DP, group_rows, FF)
        grad_all = jnp.stack(grads).reshape(MICRO, N_DP, group_rows, D)
        first_total = jnp.zeros((D, FF), jnp.float32)
        second_total = jnp.zeros((FF, D), jnp.float32)
        for group_index in range(N_DP):
            group_in = in_all[:, group_index].reshape(MICRO * group_rows, D)
            group_delta = delta_all[:, group_index].reshape(MICRO * group_rows, FF)
            group_act = act_all[:, group_index].reshape(MICRO * group_rows, FF)
            group_grad = grad_all[:, group_index].reshape(MICRO * group_rows, D)
            first_term = lax.dot_general(group_in, group_delta, (((0,), (0,)), ((), ())), preferred_element_type=jnp.float32) * factor
            second_term = lax.dot_general(group_act, group_grad, (((0,), (0,)), ((), ())), preferred_element_type=jnp.float32) * factor
            first_total = first_total + lax.optimization_barrier(first_term.astype(jnp.bfloat16)).astype(jnp.float32)
            second_total = second_total + lax.optimization_barrier(second_term.astype(jnp.bfloat16)).astype(jnp.float32)
        first_list[section] = first_total.astype(jnp.bfloat16)
        second_list[section] = second_total.astype(jnp.bfloat16)
        segment_list[section] = jnp.stack(news)
        grads = news
    return (jnp.stack(segment_list), jnp.stack(first_list), jnp.stack(second_list))
```

```python
import math

import jax
import jax.numpy as jnp
from jax import lax
from jax.sharding import PartitionSpec as P


def gelu_pair(pre_act):
    inner_arg = 0.7978845608028654 * (pre_act + 0.044715 * pre_act * pre_act * pre_act)
    tangent = jnp.tanh(inner_arg)
    gelu_value = 0.5 * pre_act * (1.0 + tangent)
    gelu_slope = 0.5 * (1.0 + tangent) + 0.5 * pre_act * (
        1.0 - tangent * tangent
    ) * 0.7978845608028654 * (1.0 + 3.0 * 0.044715 * pre_act * pre_act)
    return (gelu_value, gelu_slope)


def on_device(inputs, cotangent, w_in, w_out):
    sections = lax.axis_size("segment")
    segment = lax.axis_index("segment")
    tp_size = lax.axis_size("tp")
    dp_size = lax.axis_size("dp")
    core = lax.rem(lax.axis_index("tp"), 2)
    chips = tp_size // 2
    chip_groups = [[2 * k + c for k in range(chips)] for c in range(2)]
    partner = [(i, i ^ 1) for i in range(tp_size)]
    micro_count, rows, narrow = inputs.shape
    wide = 2 * narrow
    first_weight = w_in[0]
    second_weight = w_out[0]
    width, units = first_weight.shape

    def swap(block):
        return lax.ppermute(block, "tp", partner)

    def over_chips(blocks):
        return lax.all_to_all(blocks, "tp", 0, 0, axis_index_groups=chip_groups)

    def over_rows(blocks):
        return lax.all_to_all(blocks, "dp", 0, 0)

    def to_shard(block):
        own = lax.dynamic_index_in_dim(block, core, 0, keepdims=False)
        came = swap(lax.dynamic_index_in_dim(block, 1 - core, 0, keepdims=False))
        return jnp.where(
            core == 0,
            jnp.concatenate([own, came], axis=1),
            jnp.concatenate([came, own], axis=1),
        )

    def from_shard(shard):
        left, right = shard[:, :narrow], shard[:, narrow:]
        own = jnp.where(core == 0, left, right)
        came = swap(jnp.where(core == 0, right, left))
        return jnp.where(core == 0, jnp.stack([own, came]), jnp.stack([came, own]))

    def rows_of(blocks):
        return blocks.transpose(1, 0, 2).reshape(rows, width)

    def gather(shard):
        blocks = over_chips(jnp.broadcast_to(shard[None], (chips, rows, wide)))
        return jnp.concatenate([rows_of(blocks), rows_of(swap(blocks))], axis=0)

    def scatter(partial, shard):
        partial = partial.astype(jnp.bfloat16)
        came = swap(partial[rows:])
        paired = (partial[:rows].astype(jnp.float32) + came.astype(jnp.float32)).astype(jnp.bfloat16)
        blocks = over_chips(paired.reshape(rows, chips, wide).transpose(1, 0, 2))
        total = jnp.sum(blocks.astype(jnp.float32), axis=0)
        return (shard.astype(jnp.float32) + total).astype(jnp.bfloat16)

    def hop(shard, kept, source, target):
        came = lax.ppermute(shard, "segment", [(source, target)])
        return jnp.where(segment == target, came, kept)

    def slices(full):
        return full.reshape(2 * rows, dp_size, width // dp_size).transpose(1, 0, 2)

    def copies(block):
        return jnp.broadcast_to(block[None], (dp_size,) + block.shape)

    shard = to_shard(inputs)
    for section in range(sections):
        full_in = gather(shard)
        pre_act = jnp.dot(full_in, first_weight, preferred_element_type=jnp.float32)
        if section < sections - 1:
            activation = gelu_pair(pre_act)[0].astype(jnp.bfloat16)
            partial = jnp.dot(activation, second_weight, preferred_element_type=jnp.float32)
            shard = hop(scatter(partial, shard), shard, section, section + 1)
    activation, slope = gelu_pair(pre_act)
    all_in = over_rows(
        jnp.concatenate([slices(full_in), copies(activation.astype(jnp.bfloat16))], axis=2)
    )

    shard = to_shard(cotangent)
    for section in reversed(range(sections)):
        full_grad = gather(shard)
        upstream = lax.dot_general(
            full_grad, second_weight, (((1,), (1,)), ((), ())), preferred_element_type=jnp.float32
        )
        delta = (upstream * slope).astype(jnp.bfloat16)
        partial = lax.dot_general(
            delta, first_weight, (((1,), (1,)), ((), ())), preferred_element_type=jnp.float32
        )
        leaving = scatter(partial, shard)
        if section > 0:
            shard = hop(leaving, shard, section, section - 1)
    all_grad = over_rows(slices(full_grad))
    all_delta = over_rows(copies(delta))
    grad_scale = 1.0 / math.sqrt(micro_count * rows * dp_size)
    by_rows = (((0, 1), (0, 1)), ((), ()))
    depth = width // dp_size
    grad_first = lax.dot_general(
        all_in[:, :, :depth], all_delta, by_rows, preferred_element_type=jnp.float32
    )
    grad_second = lax.dot_general(
        all_in[:, :, depth:], all_grad, by_rows, preferred_element_type=jnp.float32
    )
    return (
        from_shard(leaving)[None, :],
        (grad_first * grad_scale).astype(jnp.bfloat16)[None],
        (grad_second * grad_scale).astype(jnp.bfloat16)[None],
    )


def solution(mesh):
    return jax.shard_map(
        on_device,
        mesh=mesh,
        in_specs=(
            P(None, "dp", "tp"),
            P(None, "dp", "tp"),
            P("segment", None, "tp"),
            P("segment", "tp", None),
        ),
        out_specs=(
            P("segment", None, "dp", "tp"),
            P("segment", "dp", "tp"),
            P("segment", "tp", "dp"),
        ),
        check_vma=False,
    )
```

```python
import math

import jax
import jax.numpy as jnp
from jax import lax
from jax.sharding import PartitionSpec as P


def gelu_pair(pre_act):
    inner_arg = 0.7978845608028654 * (pre_act + 0.044715 * pre_act * pre_act * pre_act)
    tangent = jnp.tanh(inner_arg)
    gelu_value = 0.5 * pre_act * (1.0 + tangent)
    gelu_slope = 0.5 * (1.0 + tangent) + 0.5 * pre_act * (
        1.0 - tangent * tangent
    ) * 0.7978845608028654 * (1.0 + 3.0 * 0.044715 * pre_act * pre_act)
    return (gelu_value, gelu_slope)


def on_device(inputs, cotangent, w_in, w_out):
    sections = lax.axis_size("segment")
    segment = lax.axis_index("segment")
    tp_size = lax.axis_size("tp")
    dp_size = lax.axis_size("dp")
    core = lax.rem(lax.axis_index("tp"), 2)
    chips = tp_size // 2
    chip_groups = [[2 * k + c for k in range(chips)] for c in range(2)]
    partner = [(i, i ^ 1) for i in range(tp_size)]
    micro_count, rows, narrow = inputs.shape
    wide = 2 * narrow
    first_weight = w_in[0]
    second_weight = w_out[0]
    width, units = first_weight.shape

    def swap(block):
        return lax.ppermute(block, "tp", partner)

    def over_chips(blocks):
        return lax.all_to_all(blocks, "tp", 0, 0, axis_index_groups=chip_groups)

    def to_shard(block):
        own = lax.dynamic_index_in_dim(block, core, 0, keepdims=False)
        came = swap(lax.dynamic_index_in_dim(block, 1 - core, 0, keepdims=False))
        return jnp.where(
            core == 0,
            jnp.concatenate([own, came], axis=1),
            jnp.concatenate([came, own], axis=1),
        )

    def from_shard(shard):
        left, right = shard[:, :narrow], shard[:, narrow:]
        own = jnp.where(core == 0, left, right)
        came = swap(jnp.where(core == 0, right, left))
        return jnp.where(core == 0, jnp.stack([own, came]), jnp.stack([came, own]))

    def rows_of(blocks):
        return blocks.transpose(1, 0, 2).reshape(rows, width)

    def spread(shard):
        return over_chips(jnp.broadcast_to(shard[None], (chips, rows, wide)))

    def both_halves(blocks):
        return jnp.concatenate([rows_of(blocks), rows_of(swap(blocks))], axis=0)

    def scatter(partial, shard, name):
        partial = partial.astype(jnp.bfloat16)
        came = swap(partial[rows:])
        paired = (partial[:rows].astype(jnp.float32) + came.astype(jnp.float32)).astype(jnp.bfloat16)
        with jax.named_scope(f"rs_{name}"):
            blocks = over_chips(paired.reshape(rows, chips, wide).transpose(1, 0, 2))
        total = jnp.sum(blocks.astype(jnp.float32), axis=0)
        return (shard.astype(jnp.float32) + total).astype(jnp.bfloat16)

    def hop(shard, kept, source, target, name):
        with jax.named_scope(f"hop_{name}"):
            came = lax.ppermute(shard, "segment", [(source, target)])
        return jnp.where(segment == target, came, kept)

    scope = jax.named_scope
    depth = width // dp_size

    def forward(section, state):
        shard, _, _, _ = state
        with scope(f"ag_f{section}"):
            blocks = spread(shard)
        with scope(f"swap_f{section}"):
            full_in = both_halves(blocks)
        with scope(f"mm_f{section}"):
            pre_act = jnp.dot(full_in, first_weight, preferred_element_type=jnp.float32)
            value, slope = gelu_pair(pre_act)
            activation = value.astype(jnp.bfloat16)
        if section < sections - 1:
            with scope(f"mm_f{section}"):
                partial = jnp.dot(activation, second_weight, preferred_element_type=jnp.float32)
            shard = scatter(partial, shard, f"f{section}")
        return (shard, full_in[:rows], activation, slope)

    def up(full_grad):
        return lax.dot_general(
            full_grad, second_weight, (((1,), (1,)), ((), ())), preferred_element_type=jnp.float32
        )

    def down(delta):
        return lax.dot_general(
            delta, first_weight, (((1,), (1,)), ((), ())), preferred_element_type=jnp.float32
        )

    def start_back(grad_shard):
        full_grad = both_halves(spread(grad_shard))
        return (full_grad[:rows], up(full_grad))

    def turn(operands):
        state, upstream, grad_shard = operands
        state = forward(sections - 1, state)
        delta = (upstream * state[3]).astype(jnp.bfloat16)
        return (state, scatter(down(delta), grad_shard, "turn"), delta)

    def backward(section, grad_shard, slope):
        with scope(f"ag_b{section}"):
            blocks = spread(grad_shard)
        with scope(f"swap_b{section}"):
            full_grad = both_halves(blocks)
        with scope(f"up_b{section}"):
            delta = (up(full_grad) * slope).astype(jnp.bfloat16)
        with scope(f"mm_b{section}"):
            partial = down(delta)
        return (scatter(partial, grad_shard, f"b{section}"), full_grad[:rows], delta)

    dp_index = lax.axis_index("dp")
    routes = [[(i, (i + r) % dp_size) for i in range(dp_size)] for r in range(dp_size)]

    def exchange_columns(own):
        out = [lax.dynamic_slice_in_dim(own, dp_index * depth, depth, 1)]
        for r in range(1, dp_size):
            goes = lax.rem(dp_index + r, dp_size) * depth
            out.append(lax.ppermute(lax.dynamic_slice_in_dim(own, goes, depth, 1), "dp", routes[r]))
        return jnp.concatenate(out, axis=0)

    def exchange_units(block):
        return jnp.stack([block] + [lax.ppermute(block, "dp", routes[r]) for r in range(1, dp_size)])

    def exchange(own, block):
        return exchange_columns(own), exchange_units(block)

    grad_scale = 1.0 / math.sqrt(micro_count * rows * dp_size)

    def product(left, right):
        return lax.dot_general(left, right, (((0,), (0,)), ((), ())), preferred_element_type=jnp.float32)

    def halves(blocks):
        return (
            blocks[:, :rows].reshape(dp_size * rows, units),
            blocks[:, rows:].reshape(dp_size * rows, units),
        )

    def weight_grads(all_in, all_act, all_grad, all_delta):
        act_own, act_other = halves(all_act)
        delta_own, delta_other = halves(all_delta)
        first = product(all_in, delta_own) + product(swap(all_in), delta_other)
        second = product(act_own, all_grad) + product(act_other, swap(all_grad))
        return (
            (first * grad_scale).astype(jnp.bfloat16),
            (second * grad_scale).astype(jnp.bfloat16),
        )

    grad_shard = to_shard(cotangent)
    shard = to_shard(inputs)
    nothing = lambda shape, kind: jnp.zeros(shape, kind)
    own_grad, upstream = lax.cond(
        segment == sections - 1,
        start_back,
        lambda _: (
            nothing((rows, width), jnp.bfloat16),
            nothing((2 * rows, units), jnp.float32),
        ),
        grad_shard,
    )
    state = (
        shard,
        nothing((rows, width), jnp.bfloat16),
        nothing((2 * rows, units), jnp.bfloat16),
        nothing((2 * rows, units), jnp.float32),
    )
    for section in range(sections - 1):
        state = lax.cond(
            segment == section, lambda s, k=section: forward(k, s), lambda s: s, state
        )
        shard = hop(state[0], state[0], section, section + 1, f"f{section}")
        state = (shard,) + state[1:]
    state, leaving, delta = lax.cond(
        segment == sections - 1,
        turn,
        lambda o: (o[0], o[2], nothing((2 * rows, units), jnp.bfloat16)),
        (state, upstream, grad_shard),
    )
    _, own_in, activation, slope = state
    all_in, all_act = (
        nothing((dp_size * rows, depth), jnp.bfloat16),
        nothing((dp_size, 2 * rows, units), jnp.bfloat16),
    )
    for section in reversed(range(sections - 1)):
        shard = hop(leaving, grad_shard, section + 1, section, f"b{section + 1}")
        turn_now = [segment == section + 1] if section < sections - 2 else [segment != section]
        if section >= sections - 3:
            all_in, all_act = lax.cond(
                turn_now[0],
                lambda o: exchange(o[0], o[1]),
                lambda o: (o[2], o[3]),
                (own_in, activation, all_in, all_act),
            )
        if section > 0:
            leaving, own_grad, delta = lax.cond(
                segment == section,
                lambda o, k=section: backward(k, o[0], o[1]),
                lambda o: o[2:],
                (shard, slope, leaving, own_grad, delta),
            )
            grad_shard = jnp.where(segment == section, shard, grad_shard)

    def finish(operands):
        shard, slope, all_in, all_act, _, _, _ = operands
        with scope("ag_b0"):
            blocks = spread(shard)
        own_grad = rows_of(blocks)
        all_grad = exchange_columns(own_grad)
        full_grad = jnp.concatenate([own_grad, rows_of(swap(blocks))], axis=0)
        delta = (up(full_grad) * slope).astype(jnp.bfloat16)
        all_delta = exchange_units(delta)
        leaving = scatter(down(delta), shard, "b0")
        return (leaving,) + weight_grads(all_in, all_act, all_grad, all_delta)

    def only_grads(operands):
        _, _, all_in, all_act, leaving, own_grad, delta = operands
        all_grad, all_delta = exchange(own_grad, delta)
        return (leaving,) + weight_grads(all_in, all_act, all_grad, all_delta)

    leaving, grad_first, grad_second = lax.cond(
        segment == 0,
        finish,
        only_grads,
        (shard, slope, all_in, all_act, leaving, own_grad, delta),
    )
    return (from_shard(leaving)[None, :], grad_first[None], grad_second[None])


def solution(mesh):
    return jax.shard_map(
        on_device,
        mesh=mesh,
        in_specs=(
            P(None, "dp", "tp"),
            P(None, "dp", "tp"),
            P("segment", None, "tp"),
            P("segment", "tp", None),
        ),
        out_specs=(
            P("segment", None, "dp", "tp"),
            P("segment", "dp", "tp"),
            P("segment", "tp", "dp"),
        ),
        check_vma=False,
    )
```
